128 devices in a mesh: dp: 2 (over core), expert: 32 (over x, z_hi, y), replica: 2 (over z_lo).
Axes of the slice: x: 4, y: 4, z: 4 (z_hi: 2, z_lo: 2; z = z_hi * 2 + z_lo), core: 2. Of those that a mesh axis runs over, the one named last changes fastest.
Arguments:
- tokens: bfloat16 [16384, 4096], P(('dp', 'expert', 'replica')), may hold values from -6 to 6
- expert_ids: int32 [16384, 8], P(('dp', 'expert', 'replica')), may hold values from 0 to 63, all different within a row; in each aligned block of 128 rows (0 to 127, 128 to 255, ...) at most 24 rows name the same one
- router_weight: bfloat16 [4096, 64], replicated, may hold values from -0.09375 to 0.09375
- gate_weight: bfloat16 [64, 4096, 768], P(('expert', 'replica')), may hold values from -0.09375 to 0.09375
- up_weight: bfloat16 [64, 4096, 768], P(('expert', 'replica')), may hold values from -0.09375 to 0.09375
- down_weight: bfloat16 [64, 768, 4096], P(('expert', 'replica')), may hold values from -0.21875 to 0.21875
- cotangent: bfloat16 [16384, 4096], P(('dp', 'expert', 'replica')), may hold values from -0.09375 to 0.09375
Outputs:
- mixed: bfloat16 [16384, 4096], P(('dp', 'expert', 'replica'))
- router_grad: float32 [4096, 64], replicated
The draws below stay inside these ranges and needn't reach their ends.
Inputs may be any that keep to these rules, and one draw needn't show every extreme that they name: `expert_ids`: in each aligned block of 128 rows (the rows of one device) no expert is named by more than 24 rows, and in every draw some expert is named by exactly 24 rows of some block.
All inputs are finite; a program needn't handle non-finite values.
Results may differ from the reference program's by a relative error of at most 0.0057.
Values may be sent and summed in bfloat16 or wider, within the bound.
No kernel may reach another device: no remote copies, remote signals or barrier semaphores. Data moves between devices by JAX's collectives and lax.ppermute only.
A program may use at most 128 MiB of HBM per device.

```python
import math
import jax
import jax.numpy as jnp
import numpy as np
from jax import lax

D = 4096
FFE = 768
TOPK = 8
TOK_DEV = 128
E = 64
CAP = 24
TOKENS = 16384


def levels(rng, shape, shards, smallest, largest):
    loudness, own = 1.0, jax.random.fold_in(rng, 6)
    for position, shards_of in shards:
        draws = jnp.exp(jax.random.uniform(jax.random.fold_in(own, position), (shards_of,), jnp.float32, smallest / len(shards), largest / len(shards)))
        loudness = loudness * jnp.repeat(draws, shape[position] // shards_of).reshape([-1 if axis == position else 1 for axis in range(len(shape))])
    return loudness


def routed_block(rng, own, number, rows, count, top, reach, lean):
    sequence = jax.random.permutation(rng, count)
    crowded, usual = portions_of(count, rows * top, reach, lean, True), portions_of(count, rows * top, reach, lean, False)
    places = jnp.arange(count)

    def named(lengths, turn):
        used = int((lengths > 0).sum())
        fixed = max(1, used // 4)
        moved = fixed + (places - fixed + turn * (used - fixed)) % max(1, count - fixed)
        return jnp.zeros((count,), jnp.int32).at[sequence[jnp.where(places < fixed, places, moved)]].set(jnp.asarray(lengths, jnp.int32))

    lengths = jnp.where(number % 4 == 0, named(crowded, number // 4), named(usual, number - number // 4 - 1))
    mixed = jax.random.permutation(jax.random.fold_in(own, 3), count)
    donor, receiver = mixed[0:count // 2 * 2:2], mixed[1:count // 2 * 2:2]
    margin = jnp.minimum(lengths[donor] - 1, reach - lengths[receiver]) // 2
    margin = jnp.where((donor == sequence[0]) | (receiver == sequence[0]) | (lengths[receiver] == 0), 0, jnp.maximum(margin, 0))
    moved = jax.random.randint(jax.random.fold_in(own, 4), (count // 2,), 0, 1 << 20) % (margin + 1)
    lengths = lengths.at[donor].add(-moved).at[receiver].add(moved)
    items = jnp.searchsorted(jnp.cumsum(lengths), jnp.arange(rows * top), side="right").astype(jnp.int32)
    grid = items.reshape(top, rows).T
    grid = grid[jax.random.permutation(jax.random.fold_in(own, 1), rows)]
    turn = jax.random.randint(jax.random.fold_in(own, 2), (rows, 1), 0, top)
    return jnp.take_along_axis(grid, (jnp.arange(top)[None, :] + turn) % top, axis=1)


def portions_of(amount, total, limit, slope, full):
    portions = [(1 << 20) // math.isqrt(grade ** slope) + 1 for grade in range(1, amount + 1)]
    largest = limit if full else min(limit, max(-(-total // amount), total * portions[0] // sum(portions)))
    least = 1 if total - largest >= amount - 1 else 0
    given, rest = [largest] + [least] * (amount - 1), total - largest - least * (amount - 1)
    while rest > 0:
        movable = [i for i in range(1, amount) if given[i] < largest] or [i for i in range(1, amount) if given[i] < limit]
        whole, remaining = sum([portions[i] for i in movable]), rest
        for i in movable:
            more = min(limit - given[i], max(1, remaining * portions[i] // whole), rest)
            given[i] = given[i] + more
            rest = rest - more
    return np.array(given)


def normal_values(own_key, extent, spread, bound, shards=(), dtype=jnp.bfloat16):
    values = jax.random.normal(own_key, extent, jnp.float32) * spread
    if len(shards) > 0:
        values = levels(own_key, extent, shards, -0.22, 0.18) * values
    return jnp.clip(values, min=-bound, max=bound).astype(dtype)


def setup_inputs(seed: int = 0) -> dict:
    seeds = jax.random.split(jax.random.key(seed), 8)
    tokens = normal_values(seeds[0], (TOKENS, D), 1.0, 6.0, ((0, 128),))
    expert_ids_keys = jax.random.split(jax.random.fold_in(seeds[1], 1), TOKENS // TOK_DEV)
    expert_ids_turns = jax.random.permutation(jax.random.fold_in(seeds[1], 3), TOKENS // TOK_DEV)
    expert_ids = jax.vmap(lambda own, number: routed_block(jax.random.fold_in(seeds[1], 2), own, number, TOK_DEV, E, TOPK, CAP, 2))(expert_ids_keys, expert_ids_turns).reshape((TOKENS, TOPK))
    router_weight = normal_values(seeds[2], (D, E), D ** -0.5, 0.09375)
    gate_weight = normal_values(seeds[3], (E, D, FFE), D ** -0.5, 0.09375, ((0, 64),))
    up_weight = normal_values(seeds[4], (E, D, FFE), D ** -0.5, 0.09375, ((0, 64),))
    down_weight = normal_values(seeds[5], (E, FFE, D), FFE ** -0.5, 0.21875, ((0, 64),))
    cotangent = normal_values(seeds[6], (TOKENS, D), D ** -0.5, 0.09375, ((0, 128),))
    return dict(tokens=tokens, expert_ids=expert_ids, router_weight=router_weight, gate_weight=gate_weight, up_weight=up_weight, down_weight=down_weight, cotangent=cotangent)


def reference(tokens, expert_ids, router_weight, gate_weight, up_weight, down_weight, cotangent):
    logits = jnp.dot(tokens, router_weight, preferred_element_type=jnp.float32)
    chosen = jnp.take_along_axis(logits, expert_ids, axis=1)
    raised = jnp.exp(chosen)
    gate_probs = raised / jnp.sum(raised, axis=1, keepdims=True)
    flat_ids = expert_ids.reshape(-1)
    flat_probs = gate_probs.reshape(-1)
    row_bound = (TOKENS // TOK_DEV) * CAP

    def per_expert(carry, expert):
        mixed_acc, dot_acc = carry
        matches = flat_ids == expert
        (picked_idx,) = jnp.nonzero(matches, size=row_bound, fill_value=0)
        live_mask = (jnp.arange(row_bound) < jnp.sum(matches)).astype(jnp.float32)
        token_idx = picked_idx // TOPK
        picked = tokens[token_idx]
        gate_act = jnp.dot(picked, gate_weight[expert], preferred_element_type=jnp.float32)
        up_act = jnp.dot(picked, up_weight[expert], preferred_element_type=jnp.float32)
        hidden = (jax.nn.silu(gate_act) * up_act).astype(jnp.bfloat16)
        slot_out = jnp.dot(hidden, down_weight[expert], preferred_element_type=jnp.float32).astype(jnp.bfloat16)
        out_wide = slot_out.astype(jnp.float32)
        scale_rows = flat_probs[picked_idx] * live_mask
        mixed_acc = mixed_acc.at[token_idx].add(scale_rows[:, None] * out_wide)
        dot_rows = jnp.sum(out_wide * cotangent[token_idx].astype(jnp.float32), axis=1) * live_mask
        dot_acc = dot_acc.at[picked_idx].add(dot_rows)
        return (mixed_acc, dot_acc), None

    start = (jnp.zeros((TOKENS, D), jnp.float32), jnp.zeros((TOKENS * TOPK,), jnp.float32))
    (mixed_acc, dot_acc), _ = lax.scan(per_expert, start, jnp.arange(E).astype(jnp.int32))
    mixed = mixed_acc.astype(jnp.bfloat16)
    slot_dots = dot_acc.reshape(TOKENS, TOPK)
    logit_grad = gate_probs * (slot_dots - jnp.sum(gate_probs * slot_dots, axis=1, keepdims=True))
    match_table = (expert_ids[:, :, None] == jnp.arange(E).astype(jnp.int32)[None, None, :]).astype(jnp.float32)
    grad_table = jnp.sum(match_table * logit_grad[:, :, None], axis=1)
    router_grad = jnp.dot(tokens.astype(jnp.float32).T, grad_table, precision=lax.Precision.HIGHEST)
    return mixed, router_grad
```

```python
import jax
import jax.numpy as jnp
from jax import lax
from jax.sharding import PartitionSpec as P

GROUP = ("expert", "replica")
STEP = 8


def exchange(rows):
    return lax.all_to_all(rows, GROUP, split_axis=0, concat_axis=0, tiled=True)


def expert_apply(rows, gate_mat, up_mat, down_mat):
    gate_act = jnp.dot(rows, gate_mat, preferred_element_type=jnp.float32)
    up_act = jnp.dot(rows, up_mat, preferred_element_type=jnp.float32)
    hidden = (jax.nn.silu(gate_act) * up_act).astype(jnp.bfloat16)
    return jnp.dot(hidden, down_mat, preferred_element_type=jnp.float32).astype(jnp.bfloat16)


def local(tokens, expert_ids, router_weight, gate_weight, up_weight, down_weight, cotangent):
    tok_rows, model_width = tokens.shape
    top_count = expert_ids.shape[1]
    experts = router_weight.shape[1]
    capacity = 3 * tok_rows * top_count // (2 * experts)
    ids_t = expert_ids.T
    names = jnp.arange(experts, dtype=jnp.int32)
    member = jnp.any(ids_t[:, None, :] == names[None, :, None], axis=0)
    earlier = (jnp.arange(tok_rows)[:, None] < jnp.arange(tok_rows)[None, :]).astype(jnp.bfloat16)
    before = jnp.dot(member.astype(jnp.bfloat16), earlier, preferred_element_type=jnp.float32)
    slot = jnp.where(member, before.astype(jnp.int32), -1)

    picks = []
    sent = []
    for start in range(0, capacity, STEP):
        wanted = start + jnp.arange(STEP, dtype=jnp.int32)
        pick = (slot[:, None, :] == wanted[None, :, None]).reshape(experts * STEP, tok_rows)
        box = jnp.dot(pick.astype(jnp.bfloat16), tokens, preferred_element_type=jnp.float32)
        picks.append(pick)
        sent.append(exchange(box.astype(jnp.bfloat16).reshape(experts, STEP, model_width)))

    logits = lax.dot_general(
        router_weight, tokens, (((0,), (1,)), ((), ())), preferred_element_type=jnp.float32
    )
    raised = jnp.where(member, jnp.exp(logits), 0.0)
    probs = raised / jnp.sum(raised, axis=0, keepdims=True)

    mixed = jnp.zeros((tok_rows, model_width), jnp.float32)
    dots = jnp.zeros((experts, tok_rows), jnp.float32)
    for pick, rows in zip(picks, sent):
        out = expert_apply(rows.reshape(-1, model_width), gate_weight[0], up_weight[0], down_weight[0])
        back = exchange(out.reshape(experts, STEP, model_width)).reshape(-1, model_width)
        every = lax.dot_general(
            back, cotangent, (((1,), (1,)), ((), ())), preferred_element_type=jnp.float32
        )
        dots = dots + jnp.sum(jnp.where(pick, every, 0.0).reshape(experts, STEP, tok_rows), axis=1)
        share = jnp.where(
            pick.reshape(experts, STEP, tok_rows), probs[:, None, :], 0.0
        ).astype(jnp.bfloat16).reshape(-1, tok_rows)
        mixed = mixed + lax.dot_general(
            share, back, (((0,), (0,)), ((), ())), preferred_element_type=jnp.float32
        )
    table = probs * (dots - jnp.sum(probs * dots, axis=0, keepdims=True))
    grad = jnp.dot(table, tokens.astype(jnp.float32), precision=lax.Precision.HIGHEST)
    row = jnp.sum(exchange(grad), axis=0, keepdims=True)
    row = row + lax.ppermute(row, "dp", [(0, 1), (1, 0)])
    router_grad = exchange(jnp.broadcast_to(row, (experts, model_width)))
    return (mixed.astype(jnp.bfloat16), router_grad.T)


def solution(mesh):
    in_specs = (
        P(("dp", "expert", "replica"), None),
        P(("dp", "expert", "replica"), None),
        P(),
        P(("expert", "replica"), None, None),
        P(("expert", "replica"), None, None),
        P(("expert", "replica"), None, None),
        P(("dp", "expert", "replica"), None),
    )
    out_specs = (P(("dp", "expert", "replica"), None), P())
    return jax.shard_map(local, mesh=mesh, in_specs=in_specs, out_specs=out_specs, check_vma=False)
```

```python
import jax
import jax.numpy as jnp
from jax import lax
from jax.sharding import PartitionSpec as P

GROUP = ("expert", "replica")


def exchange(rows):
    return lax.all_to_all(rows, GROUP, split_axis=0, concat_axis=0, tiled=True)


def expert_apply(rows, gate_mat, up_mat, down_mat):
    gate_act = jnp.dot(rows, gate_mat, preferred_element_type=jnp.float32)
    up_act = jnp.dot(rows, up_mat, preferred_element_type=jnp.float32)
    hidden = (jax.nn.silu(gate_act) * up_act).astype(jnp.bfloat16)
    return jnp.dot(hidden, down_mat, preferred_element_type=jnp.float32).astype(jnp.bfloat16)


def local(tokens, expert_ids, router_weight, gate_weight, up_weight, down_weight, cotangent):
    tok_rows, model_width = tokens.shape
    top_count = expert_ids.shape[1]
    experts = router_weight.shape[1]
    capacity = 3 * tok_rows * top_count // (2 * experts)
    ids_t = expert_ids.T
    names = jnp.arange(experts, dtype=jnp.int32)
    member = jnp.any(ids_t[:, None, :] == names[None, :, None], axis=0)
    earlier = (jnp.arange(tok_rows)[:, None] < jnp.arange(tok_rows)[None, :]).astype(jnp.bfloat16)
    before = jnp.dot(member.astype(jnp.bfloat16), earlier, preferred_element_type=jnp.float32)
    slot = jnp.where(member, before.astype(jnp.int32), -1)

    wanted = jnp.arange(capacity, dtype=jnp.int32)
    pick = slot[:, None, :] == wanted[None, :, None]
    logits = lax.dot_general(
        router_weight, tokens, (((0,), (1,)), ((), ())), preferred_element_type=jnp.float32
    )
    raised = jnp.where(member, jnp.exp(logits), 0.0)
    probs = raised / jnp.sum(raised, axis=0, keepdims=True)
    box = jnp.dot(
        pick.reshape(-1, tok_rows).astype(jnp.bfloat16), tokens, preferred_element_type=jnp.float32
    ).astype(jnp.bfloat16)
    box, probs, slot = lax.optimization_barrier((box, probs, slot))

    rows = exchange(box.reshape(experts, capacity, model_width)).reshape(-1, model_width)
    out = expert_apply(rows, gate_weight[0], up_weight[0], down_weight[0])
    back = exchange(out.reshape(experts, capacity, model_width)).reshape(-1, model_width)

    pick = slot[:, None, :] == wanted[None, :, None]
    every = lax.dot_general(
        back, cotangent, (((1,), (1,)), ((), ())), preferred_element_type=jnp.float32
    ).reshape(experts, capacity, tok_rows)
    dots = jnp.sum(jnp.where(pick, every, 0.0), axis=1)
    table = probs * (dots - jnp.sum(probs * dots, axis=0, keepdims=True))
    slot_grad = jnp.sum(jnp.where(pick, table[:, None, :], 0.0), axis=2)
    theirs = exchange(slot_grad[:, None, :])
    share = jnp.where(pick, probs[:, None, :], 0.0).astype(jnp.bfloat16).reshape(-1, tok_rows)
    mixed = lax.dot_general(
        share, back, (((0,), (0,)), ((), ())), preferred_element_type=jnp.float32
    ).astype(jnp.bfloat16)
    row = jnp.sum(rows.astype(jnp.float32) * theirs.reshape(-1, 1), axis=0, keepdims=True)
    row = row + lax.ppermute(row, "dp", [(0, 1), (1, 0)])
    columns = exchange(jnp.broadcast_to(row.astype(jnp.bfloat16), (experts, model_width)))
    return (mixed, columns.astype(jnp.float32).T)


def solution(mesh):
    in_specs = (
        P(("dp", "expert", "replica"), None),
        P(("dp", "expert", "replica"), None),
        P(),
        P(("expert", "replica"), None, None),
        P(("expert", "replica"), None, None),
        P(("expert", "replica"), None, None),
        P(("dp", "expert", "replica"), None),
    )
    out_specs = (P(("dp", "expert", "replica"), None), P())
    return jax.shard_map(local, mesh=mesh, in_specs=in_specs, out_specs=out_specs, check_vma=False)
```

```python
import jax
import jax.numpy as jnp
from jax import lax
from jax.experimental import pallas as pl
from jax.experimental.pallas import tpu as pltpu
from jax.sharding import PartitionSpec as P

GROUP = ("expert", "replica")
TILE = 256
SPAN = 1024
GROUPED = 8


def exchange(rows):
    return lax.all_to_all(rows, GROUP, split_axis=0, concat_axis=0, tiled=True)


def expert_kernel(rows_ref, gate_hbm, up_hbm, down_hbm, out_ref, gate_mat, up_mat, down_mat, sems):
    copies = [
        pltpu.make_async_copy(source, target, sems.at[n])
        for n, (source, target) in enumerate(
            ((gate_hbm, gate_mat), (up_hbm, up_mat), (down_hbm, down_mat))
        )
    ]
    first = pl.program_id(0) == 0

    @pl.when(first)
    def _():
        for copy in copies:
            copy.start()
        copies[0].wait()

    gate_act = jnp.dot(rows_ref[...], gate_mat[...], preferred_element_type=jnp.float32)

    @pl.when(first)
    def _():
        copies[1].wait()

    up_act = jnp.dot(rows_ref[...], up_mat[...], preferred_element_type=jnp.float32)
    hidden = (jax.nn.silu(gate_act) * up_act).astype(jnp.bfloat16)

    @pl.when(first)
    def _():
        copies[2].wait()

    width = out_ref.shape[1]
    for start in range(0, width, SPAN):
        part = jnp.dot(hidden, down_mat[:, start : start + SPAN], preferred_element_type=jnp.float32)
        out_ref[:, start : start + SPAN] = part.astype(jnp.bfloat16)


def expert_apply(rows, gate_mat, up_mat, down_mat):
    count, width = rows.shape
    depth = gate_mat.shape[1]
    whole = pl.BlockSpec(memory_space=pl.ANY)
    tile = pl.BlockSpec((TILE, width), lambda i: (i, 0))
    return pl.pallas_call(
        expert_kernel,
        out_shape=jax.ShapeDtypeStruct((count, width), jnp.bfloat16),
        grid=(count // TILE,),
        in_specs=[tile, whole, whole, whole],
        out_specs=tile,
        scratch_shapes=[
            pltpu.VMEM((width, depth), jnp.bfloat16),
            pltpu.VMEM((width, depth), jnp.bfloat16),
            pltpu.VMEM((depth, width), jnp.bfloat16),
            pltpu.SemaphoreType.DMA((3,)),
        ],
        compiler_params=pltpu.CompilerParams(vmem_limit_bytes=60 << 20),
        name="experts",
    )(rows, gate_mat, up_mat, down_mat)


def column_kernel(rows_ref, scale_ref, out_ref, total):
    step = pl.program_id(0)

    @pl.when(step == 0)
    def _():
        total[...] = jnp.zeros_like(total)

    blocks, slots, width = rows_ref.shape
    scales = [jnp.broadcast_to(scale_ref[s][:, None], (slots, 128)) for s in range(blocks)]
    for start in range(0, width, 128):
        part = total[:, start : start + 128]
        for s in range(blocks):
            part = part + rows_ref[s, :, start : start + 128].astype(jnp.float32) * scales[s]
        total[:, start : start + 128] = part

    @pl.when(step == pl.num_programs(0) - 1)
    def _():
        for n in range(width // 128):
            out_ref[n : n + 1, :] = jnp.sum(total[:, n * 128 : n * 128 + 128], axis=0, keepdims=True)


def column_of(rows, scales):
    sources, slots, width = rows.shape
    return pl.pallas_call(
        column_kernel,
        out_shape=jax.ShapeDtypeStruct((width // 128, 128), jnp.float32),
        grid=(sources // GROUPED,),
        in_specs=[
            pl.BlockSpec((GROUPED, slots, width), lambda i: (i, 0, 0)),
            pl.BlockSpec((GROUPED, slots), lambda i: (i, 0)),
        ],
        out_specs=pl.BlockSpec((width // 128, 128), lambda i: (0, 0)),
        scratch_shapes=[pltpu.VMEM((slots, width), jnp.float32)],
        compiler_params=pltpu.CompilerParams(vmem_limit_bytes=60 << 20),
        name="column",
    )(rows, scales)


def table_kernel(back_ref, cotangent_ref, slot_ref, probs_ref, out_ref, dots):
    step = pl.program_id(0)
    blocks, slots, width = back_ref.shape
    rows = cotangent_ref.shape[0]
    every = lax.dot_general(
        back_ref[...].reshape(blocks * slots, width),
        cotangent_ref[...],
        (((1,), (1,)), ((), ())),
        preferred_element_type=jnp.float32,
    ).reshape(blocks, slots, rows)
    wanted = lax.broadcasted_iota(jnp.int32, (blocks, slots, rows), 1)
    pick = slot_ref[...][:, None, :] == wanted
    dots[pl.ds(pl.multiple_of(step * blocks, blocks), blocks), :] = jnp.sum(
        jnp.where(pick, every, 0.0), axis=1
    )

    @pl.when(step == pl.num_programs(0) - 1)
    def _():
        probs = probs_ref[...]
        values = dots[...]
        out_ref[...] = probs * (values - jnp.sum(probs * values, axis=0, keepdims=True))


def table_of(back, cotangent, slot, probs):
    experts, slots, width = back.shape
    rows = cotangent.shape[0]
    return pl.pallas_call(
        table_kernel,
        out_shape=jax.ShapeDtypeStruct((experts, rows), jnp.float32),
        grid=(experts // GROUPED,),
        in_specs=[
            pl.BlockSpec((GROUPED, slots, width), lambda i: (i, 0, 0)),
            pl.BlockSpec((rows, width), lambda i: (0, 0)),
            pl.BlockSpec((GROUPED, rows), lambda i: (i, 0)),
            pl.BlockSpec((experts, rows), lambda i: (0, 0)),
        ],
        out_specs=pl.BlockSpec((experts, rows), lambda i: (0, 0)),
        scratch_shapes=[pltpu.VMEM((experts, rows), jnp.float32)],
        compiler_params=pltpu.CompilerParams(vmem_limit_bytes=60 << 20),
        name="table",
    )(back, cotangent, slot, probs)


def local(tokens, expert_ids, router_weight, gate_weight, up_weight, down_weight, cotangent):
    tok_rows, model_width = tokens.shape
    top_count = expert_ids.shape[1]
    experts = router_weight.shape[1]
    capacity = 3 * tok_rows * top_count // (2 * experts)
    ids_t = expert_ids.T
    names = jnp.arange(experts, dtype=jnp.int32)
    member = jnp.any(ids_t[:, None, :] == names[None, :, None], axis=0)
    earlier = (jnp.arange(tok_rows)[:, None] < jnp.arange(tok_rows)[None, :]).astype(jnp.bfloat16)
    before = jnp.dot(member.astype(jnp.bfloat16), earlier, preferred_element_type=jnp.float32)
    slot = jnp.where(member, before.astype(jnp.int32), -1)

    wanted = jnp.arange(capacity, dtype=jnp.int32)
    pick = slot[:, None, :] == wanted[None, :, None]
    logits = lax.dot_general(
        router_weight, tokens, (((0,), (1,)), ((), ())), preferred_element_type=jnp.float32
    )
    raised = jnp.where(member, jnp.exp(logits), 0.0)
    probs = raised / jnp.sum(raised, axis=0, keepdims=True)
    box = jnp.dot(
        pick.reshape(-1, tok_rows).astype(jnp.bfloat16), tokens, preferred_element_type=jnp.float32
    ).astype(jnp.bfloat16)
    box, probs, slot = lax.optimization_barrier((box, probs, slot))

    rows = exchange(box.reshape(experts, capacity, model_width)).reshape(-1, model_width)
    out = expert_apply(rows, gate_weight[0], up_weight[0], down_weight[0])
    back = exchange(out.reshape(experts, capacity, model_width)).reshape(-1, model_width)

    pick = slot[:, None, :] == wanted[None, :, None]
    table = table_of(back.reshape(experts, capacity, model_width), cotangent, slot, probs)
    slot_grad = jnp.sum(jnp.where(pick, table[:, None, :], 0.0), axis=2)
    theirs = exchange(slot_grad[:, None, :])
    share = jnp.where(pick, probs[:, None, :], 0.0).astype(jnp.bfloat16).reshape(-1, tok_rows)
    mixed = lax.dot_general(
        share, back, (((0,), (0,)), ((), ())), preferred_element_type=jnp.float32
    ).astype(jnp.bfloat16)
    column = column_of(rows.reshape(experts, capacity, model_width), theirs.reshape(experts, capacity))
    column = column + lax.ppermute(column, "dp", [(0, 1), (1, 0)])
    columns = exchange(jnp.broadcast_to(column.astype(jnp.bfloat16), (experts,) + column.shape))
    columns = columns.reshape(experts, model_width)
    return (mixed, columns.astype(jnp.float32).T)


def solution(mesh):
    in_specs = (
        P(("dp", "expert", "replica"), None),
        P(("dp", "expert", "replica"), None),
        P(),
        P(("expert", "replica"), None, None),
        P(("expert", "replica"), None, None),
        P(("expert", "replica"), None, None),
        P(("dp", "expert", "replica"), None),
    )
    out_specs = (P(("dp", "expert", "replica"), None), P())
    return jax.shard_map(local, mesh=mesh, in_specs=in_specs, out_specs=out_specs, check_vma=False)
```

```python
import jax
import jax.numpy as jnp
from jax import lax
from jax.experimental import pallas as pl
from jax.experimental.pallas import tpu as pltpu
from jax.sharding import PartitionSpec as P

GROUP = ("expert", "replica")
TILE = 384
SPAN = 512
GROUPED = 32
PIECES = 16
SPANM = 2048


def exchange(rows):
    return lax.all_to_all(rows, GROUP, split_axis=0, concat_axis=0, tiled=True)


def expert_kernel(rows_ref, gate_hbm, up_hbm, down_hbm, out_ref, gate_mat, up_mat, down_mat, sems):
    copies = [
        pltpu.make_async_copy(source, target, sems.at[n])
        for n, (source, target) in enumerate(
            ((gate_hbm, gate_mat), (up_hbm, up_mat), (down_hbm, down_mat))
        )
    ]
    first = pl.program_id(0) == 0

    @pl.when(first)
    def _():
        for copy in copies:
            copy.start()
        copies[0].wait()

    gate_act = jnp.dot(rows_ref[...], gate_mat[...], preferred_element_type=jnp.float32)

    @pl.when(first)
    def _():
        copies[1].wait()

    up_act = jnp.dot(rows_ref[...], up_mat[...], preferred_element_type=jnp.float32)
    hidden = (jax.nn.silu(gate_act) * up_act).astype(jnp.bfloat16)

    @pl.when(first)
    def _():
        copies[2].wait()

    width = out_ref.shape[1]
    for start in range(0, width, SPAN):
        part = jnp.dot(hidden, down_mat[:, start : start + SPAN], preferred_element_type=jnp.float32)
        out_ref[:, start : start + SPAN] = part.astype(jnp.bfloat16)


def expert_apply(rows, gate_mat, up_mat, down_mat):
    count, width = rows.shape
    depth = gate_mat.shape[1]
    whole = pl.BlockSpec(memory_space=pl.ANY)
    tile = pl.BlockSpec((TILE, width), lambda i: (i, 0))
    return pl.pallas_call(
        expert_kernel,
        out_shape=jax.ShapeDtypeStruct((count, width), jnp.bfloat16),
        grid=(count // TILE,),
        in_specs=[tile, whole, whole, whole],
        out_specs=tile,
        scratch_shapes=[
            pltpu.VMEM((width, depth), jnp.bfloat16),
            pltpu.VMEM((width, depth), jnp.bfloat16),
            pltpu.VMEM((depth, width), jnp.bfloat16),
            pltpu.SemaphoreType.DMA((3,)),
        ],
        compiler_params=pltpu.CompilerParams(vmem_limit_bytes=60 << 20),
        name="experts",
    )(rows, gate_mat, up_mat, down_mat)


def fetch(source, target, sems):
    count = source.shape[0] // PIECES
    copies = []
    for n in range(PIECES):
        cut = pl.ds(n * count, count)
        copies.append(pltpu.make_async_copy(source.at[cut], target.at[cut], sems.at[n]))
    for copy in copies:
        copy.start()
    return count, copies


def column_kernel(rows_hbm, scale_ref, out_ref, rows, total, sems):
    count, copies = fetch(rows_hbm, rows, sems)
    _, slots, width = rows.shape
    for n, copy in enumerate(copies):
        scales = [
            jnp.broadcast_to(scale_ref[s][:, None], (slots, 128))
            for s in range(n * count, n * count + count)
        ]
        copy.wait()
        for start in range(0, width, 128):
            lanes = slice(start, start + 128)
            part = [
                rows[n * count + s, :, lanes].astype(jnp.float32) * scales[s] for s in range(count)
            ]
            while len(part) > 1:
                part = [a + b for a, b in zip(part[::2], part[1::2])]
            if n == 0:
                total[:, lanes] = part[0]
            elif n < PIECES - 1:
                total[:, lanes] += part[0]
            else:
                out_ref[start // 128 : start // 128 + 1, :] = jnp.sum(
                    total[:, lanes] + part[0], axis=0, keepdims=True
                )


def column_of(rows, scales):
    _, slots, width = rows.shape
    near = pl.BlockSpec(memory_space=pltpu.VMEM)
    return pl.pallas_call(
        column_kernel,
        out_shape=jax.ShapeDtypeStruct((width // 128, 128), jnp.float32),
        in_specs=[pl.BlockSpec(memory_space=pl.ANY), near],
        out_specs=near,
        scratch_shapes=[
            pltpu.VMEM(rows.shape, jnp.bfloat16),
            pltpu.VMEM((slots, width), jnp.float32),
            pltpu.SemaphoreType.DMA((PIECES,)),
        ],
        compiler_params=pltpu.CompilerParams(vmem_limit_bytes=60 << 20),
        name="column",
    )(rows, scales)


def table_kernel(back_ref, cotangent_ref, slot_ref, probs_ref, out_ref, dots):
    step = pl.program_id(0)
    blocks, slots, width = back_ref.shape
    rows = cotangent_ref.shape[0]
    every = lax.dot_general(
        back_ref[...].reshape(blocks * slots, width),
        cotangent_ref[...],
        (((1,), (1,)), ((), ())),
        preferred_element_type=jnp.float32,
    ).reshape(blocks, slots, rows)
    wanted = lax.broadcasted_iota(jnp.int32, (blocks, slots, rows), 1)
    pick = slot_ref[...][:, None, :] == wanted
    dots[pl.ds(pl.multiple_of(step * blocks, blocks), blocks), :] = jnp.sum(
        jnp.where(pick, every, 0.0), axis=1
    )

    @pl.when(step == pl.num_programs(0) - 1)
    def _():
        probs = probs_ref[...]
        values = dots[...]
        out_ref[...] = probs * (values - jnp.sum(probs * values, axis=0, keepdims=True))


def table_of(back, cotangent, slot, probs):
    experts, slots, width = back.shape
    rows = cotangent.shape[0]
    return pl.pallas_call(
        table_kernel,
        out_shape=jax.ShapeDtypeStruct((experts, rows), jnp.float32),
        grid=(experts // GROUPED,),
        in_specs=[
            pl.BlockSpec((GROUPED, slots, width), lambda i: (i, 0, 0)),
            pl.BlockSpec((rows, width), lambda i: (0, 0)),
            pl.BlockSpec((GROUPED, rows), lambda i: (i, 0)),
            pl.BlockSpec((experts, rows), lambda i: (0, 0)),
        ],
        out_specs=pl.BlockSpec((experts, rows), lambda i: (0, 0)),
        scratch_shapes=[pltpu.VMEM((experts, rows), jnp.float32)],
        compiler_params=pltpu.CompilerParams(vmem_limit_bytes=60 << 20),
        name="table",
    )(back, cotangent, slot, probs)


def mixed_kernel(back_ref, slot_ref, probs_ref, out_ref, share):
    blocks, slots, width = back_ref.shape
    rows = out_ref.shape[0]

    @pl.when(pl.program_id(0) == 0)
    def _():
        wanted = lax.broadcasted_iota(jnp.int32, (blocks, slots, rows), 1)
        pick = slot_ref[...][:, None, :] == wanted
        chosen = jnp.where(pick, probs_ref[...][:, None, :], 0.0)
        share[...] = chosen.reshape(blocks * slots, rows).T.astype(jnp.bfloat16)

    out_ref[...] = jnp.dot(
        share[...], back_ref[...].reshape(blocks * slots, width), preferred_element_type=jnp.float32
    ).astype(jnp.bfloat16)


def mixed_of(back, slot, probs):
    experts, slots, width = back.shape
    rows = slot.shape[1]
    return pl.pallas_call(
        mixed_kernel,
        out_shape=jax.ShapeDtypeStruct((rows, width), jnp.bfloat16),
        grid=(width // SPANM,),
        in_specs=[
            pl.BlockSpec((experts, slots, SPANM), lambda i: (0, 0, i)),
            pl.BlockSpec((experts, rows), lambda i: (0, 0)),
            pl.BlockSpec((experts, rows), lambda i: (0, 0)),
        ],
        out_specs=pl.BlockSpec((rows, SPANM), lambda i: (0, i)),
        scratch_shapes=[pltpu.VMEM((rows, experts * slots), jnp.bfloat16)],
        compiler_params=pltpu.CompilerParams(vmem_limit_bytes=60 << 20),
        name="mixed",
    )(back, slot, probs)


def local(tokens, expert_ids, router_weight, gate_weight, up_weight, down_weight, cotangent):
    tok_rows, model_width = tokens.shape
    top_count = expert_ids.shape[1]
    experts = router_weight.shape[1]
    capacity = 3 * tok_rows * top_count // (2 * experts)
    ids_t = expert_ids.T
    names = jnp.arange(experts, dtype=jnp.int32)
    member = jnp.any(ids_t[:, None, :] == names[None, :, None], axis=0)
    earlier = (jnp.arange(tok_rows)[:, None] < jnp.arange(tok_rows)[None, :]).astype(jnp.bfloat16)
    before = jnp.dot(member.astype(jnp.bfloat16), earlier, preferred_element_type=jnp.float32)
    slot = jnp.where(member, before.astype(jnp.int32), -1)

    wanted = jnp.arange(capacity, dtype=jnp.int32)
    pick = slot[:, None, :] == wanted[None, :, None]
    logits = lax.dot_general(
        router_weight, tokens, (((0,), (1,)), ((), ())), preferred_element_type=jnp.float32
    )
    raised = jnp.where(member, jnp.exp(logits), 0.0)
    probs = raised / jnp.sum(raised, axis=0, keepdims=True)
    box = jnp.dot(
        pick.reshape(-1, tok_rows).astype(jnp.bfloat16), tokens, preferred_element_type=jnp.float32
    ).astype(jnp.bfloat16)
    box, probs, slot = lax.optimization_barrier((box, probs, slot))

    rows = exchange(box.reshape(experts, capacity, model_width)).reshape(-1, model_width)
    out = expert_apply(rows, gate_weight[0], up_weight[0], down_weight[0])
    back = exchange(out.reshape(experts, capacity, model_width)).reshape(-1, model_width)

    pick = slot[:, None, :] == wanted[None, :, None]
    table = table_of(back.reshape(experts, capacity, model_width), cotangent, slot, probs)
    slot_grad = jnp.sum(jnp.where(pick, table[:, None, :], 0.0), axis=2)
    theirs = exchange(slot_grad[:, None, :])
    mixed = mixed_of(back.reshape(experts, capacity, model_width), slot, probs)
    column = column_of(rows.reshape(experts, capacity, model_width), theirs.reshape(experts, capacity))
    column = column + lax.ppermute(column, "dp", [(0, 1), (1, 0)])
    columns = exchange(jnp.broadcast_to(column.astype(jnp.bfloat16), (experts,) + column.shape))
    columns = columns.reshape(experts, model_width)
    return (mixed, columns.astype(jnp.float32).T)


def solution(mesh):
    in_specs = (
        P(("dp", "expert", "replica"), None),
        P(("dp", "expert", "replica"), None),
        P(),
        P(("expert", "replica"), None, None),
        P(("expert", "replica"), None, None),
        P(("expert", "replica"), None, None),
        P(("dp", "expert", "replica"), None),
    )
    out_specs = (P(("dp", "expert", "replica"), None), P())
    return jax.shard_map(local, mesh=mesh, in_specs=in_specs, out_specs=out_specs, check_vma=False)
```

```python
import jax
import jax.numpy as jnp
from jax import lax
from jax.experimental import pallas as pl
from jax.experimental.pallas import tpu as pltpu
from jax.sharding import PartitionSpec as P

GROUP = ("expert", "replica")
EARLY = 16
BLOCKS = 32
SPAN = 512
GROUPED = 32
PIECES = 16
SPANM = 2048


def exchange(rows):
    return lax.all_to_all(rows, GROUP, split_axis=0, concat_axis=0, tiled=True)


def expert_kernel(rows_ref, gate_hbm, up_hbm, down_hbm, *rest):
    out_ref, gate_mat, up_mat, down_mat, sems = rest[-5:]
    copies = [
        pltpu.make_async_copy(source, target, sems.at[n])
        for n, (source, target) in enumerate(
            ((gate_hbm, gate_mat), (up_hbm, up_mat), (down_hbm, down_mat))
        )
    ]
    first = pl.program_id(0) == 0

    @pl.when(first)
    def _():
        for copy in copies:
            copy.start()
        copies[0].wait()

    blocks, slots, width = rows_ref.shape
    flat = (blocks * slots, width)
    gate_act = jnp.dot(
        rows_ref[...].reshape(flat), gate_mat[...], preferred_element_type=jnp.float32
    )

    @pl.when(first)
    def _():
        copies[1].wait()

    up_act = jnp.dot(rows_ref[...].reshape(flat), up_mat[...], preferred_element_type=jnp.float32)
    hidden = (jax.nn.silu(gate_act) * up_act).astype(jnp.bfloat16)

    @pl.when(first)
    def _():
        copies[2].wait()

    for start in range(0, width, SPAN):
        part = jnp.dot(hidden, down_mat[:, start : start + SPAN], preferred_element_type=jnp.float32)
        out_ref[:, :, start : start + SPAN] = part.astype(jnp.bfloat16).reshape(blocks, slots, SPAN)


def expert_apply(rows, gate_mat, up_mat, down_mat, capacity, place, into=None):
    sources, slots, width = rows.shape
    depth = gate_mat.shape[1]
    whole = pl.BlockSpec(memory_space=pl.ANY)
    held = [] if into is None else [into]
    return pl.pallas_call(
        expert_kernel,
        out_shape=jax.ShapeDtypeStruct((sources, capacity, width), jnp.bfloat16),
        grid=(sources // BLOCKS,),
        in_specs=[pl.BlockSpec((BLOCKS, slots, width), lambda i: (i, 0, 0)), whole, whole, whole]
        + [whole] * len(held),
        out_specs=pl.BlockSpec((BLOCKS, slots, width), lambda i: (i, place, 0)),
        scratch_shapes=[
            pltpu.VMEM((width, depth), jnp.bfloat16),
            pltpu.VMEM((width, depth), jnp.bfloat16),
            pltpu.VMEM((depth, width), jnp.bfloat16),
            pltpu.SemaphoreType.DMA((3,)),
        ],
        input_output_aliases={4: 0} if held else {},
        compiler_params=pltpu.CompilerParams(vmem_limit_bytes=60 << 20),
        cost_estimate=pl.CostEstimate(
            flops=6 * sources * slots * width * depth,
            bytes_accessed=2 * (2 * sources * slots * width + 3 * width * depth),
            transcendentals=sources * slots * depth,
        ),
        name="experts",
    )(rows, gate_mat, up_mat, down_mat, *held)


def column_kernel(early_hbm, late_hbm, scale_ref, out_ref, early, late, total, sems):
    count = early.shape[0] // PIECES
    parts = ((early_hbm, early), (late_hbm, late))
    copies = []
    for n in range(PIECES):
        cut = pl.ds(n * count, count)
        copies.append(
            [
                pltpu.make_async_copy(source.at[cut], target.at[cut], sems.at[k, n])
                for k, (source, target) in enumerate(parts)
            ]
        )
    for pair in copies:
        for copy in pair:
            copy.start()
    first = early.shape[1]
    slots = first + late.shape[1]
    width = early.shape[2]
    for n, pair in enumerate(copies):
        scales = [
            jnp.broadcast_to(scale_ref[s][:, None], (slots, 128))
            for s in range(n * count, n * count + count)
        ]
        for copy in pair:
            copy.wait()
        for start in range(0, width, 128):
            lanes = slice(start, start + 128)
            part = []
            for s in range(count):
                row = n * count + s
                part.append(early[row, :, lanes].astype(jnp.float32) * scales[s][:first])
            while len(part) > 1:
                part = [a + b for a, b in zip(part[::2], part[1::2])]
            part = [part[0][k : k + 8] for k in range(0, first, 8)]
            for s in range(count):
                row = n * count + s
                part.append(late[row, :, lanes].astype(jnp.float32) * scales[s][first:])
            part = sum(part[1:], part[0])
            if n == 0:
                total[:, lanes] = part
            elif n < PIECES - 1:
                total[:, lanes] += part
            else:
                out_ref[start // 128 : start // 128 + 1, :] = jnp.sum(
                    total[:, lanes] + part, axis=0, keepdims=True
                )


def column_of(early, late, scales):
    width = early.shape[2]
    near = pl.BlockSpec(memory_space=pltpu.VMEM)
    whole = pl.BlockSpec(memory_space=pl.ANY)
    return pl.pallas_call(
        column_kernel,
        out_shape=jax.ShapeDtypeStruct((width // 128, 128), jnp.float32),
        in_specs=[whole, whole, near],
        out_specs=near,
        scratch_shapes=[
            pltpu.VMEM(early.shape, jnp.bfloat16),
            pltpu.VMEM(late.shape, jnp.bfloat16),
            pltpu.VMEM((late.shape[1], width), jnp.float32),
            pltpu.SemaphoreType.DMA((2, PIECES)),
        ],
        compiler_params=pltpu.CompilerParams(vmem_limit_bytes=60 << 20),
        name="column",
    )(early, late, scales)


def table_kernel(back_ref, cotangent_ref, slot_ref, probs_ref, out_ref, dots):
    step = pl.program_id(0)
    blocks, slots, width = back_ref.shape
    rows = cotangent_ref.shape[0]
    every = lax.dot_general(
        back_ref[...].reshape(blocks * slots, width),
        cotangent_ref[...],
        (((1,), (1,)), ((), ())),
        preferred_element_type=jnp.float32,
    ).reshape(blocks, slots, rows)
    wanted = lax.broadcasted_iota(jnp.int32, (blocks, slots, rows), 1)
    pick = slot_ref[...][:, None, :] == wanted
    dots[pl.ds(pl.multiple_of(step * blocks, blocks), blocks), :] = jnp.sum(
        jnp.where(pick, every, 0.0), axis=1
    )

    @pl.when(step == pl.num_programs(0) - 1)
    def _():
        probs = probs_ref[...]
        values = dots[...]
        out_ref[...] = probs * (values - jnp.sum(probs * values, axis=0, keepdims=True))


def table_of(back, cotangent, slot, probs):
    experts, slots, width = back.shape
    rows = cotangent.shape[0]
    return pl.pallas_call(
        table_kernel,
        out_shape=jax.ShapeDtypeStruct((experts, rows), jnp.float32),
        grid=(experts // GROUPED,),
        in_specs=[
            pl.BlockSpec((GROUPED, slots, width), lambda i: (i, 0, 0)),
            pl.BlockSpec((rows, width), lambda i: (0, 0)),
            pl.BlockSpec((GROUPED, rows), lambda i: (i, 0)),
            pl.BlockSpec((experts, rows), lambda i: (0, 0)),
        ],
        out_specs=pl.BlockSpec((experts, rows), lambda i: (0, 0)),
        scratch_shapes=[pltpu.VMEM((experts, rows), jnp.float32)],
        compiler_params=pltpu.CompilerParams(vmem_limit_bytes=60 << 20),
        name="table",
    )(back, cotangent, slot, probs)


def mixed_kernel(back_ref, slot_ref, probs_ref, out_ref, share):
    blocks, slots, width = back_ref.shape
    rows = out_ref.shape[0]

    @pl.when(pl.program_id(0) == 0)
    def _():
        wanted = lax.broadcasted_iota(jnp.int32, (blocks, slots, rows), 1)
        pick = slot_ref[...][:, None, :] == wanted
        chosen = jnp.where(pick, probs_ref[...][:, None, :], 0.0)
        share[...] = chosen.reshape(blocks * slots, rows).T.astype(jnp.bfloat16)

    out_ref[...] = jnp.dot(
        share[...], back_ref[...].reshape(blocks * slots, width), preferred_element_type=jnp.float32
    ).astype(jnp.bfloat16)


def mixed_of(back, slot, probs):
    experts, slots, width = back.shape
    rows = slot.shape[1]
    return pl.pallas_call(
        mixed_kernel,
        out_shape=jax.ShapeDtypeStruct((rows, width), jnp.bfloat16),
        grid=(width // SPANM,),
        in_specs=[
            pl.BlockSpec((experts, slots, SPANM), lambda i: (0, 0, i)),
            pl.BlockSpec((experts, rows), lambda i: (0, 0)),
            pl.BlockSpec((experts, rows), lambda i: (0, 0)),
        ],
        out_specs=pl.BlockSpec((rows, SPANM), lambda i: (0, i)),
        scratch_shapes=[pltpu.VMEM((rows, experts * slots), jnp.bfloat16)],
        compiler_params=pltpu.CompilerParams(vmem_limit_bytes=60 << 20),
        name="mixed",
    )(back, slot, probs)


def local(tokens, expert_ids, router_weight, gate_weight, up_weight, down_weight, cotangent):
    tok_rows, model_width = tokens.shape
    top_count = expert_ids.shape[1]
    experts = router_weight.shape[1]
    capacity = 3 * tok_rows * top_count // (2 * experts)
    ids_t = expert_ids.T
    names = jnp.arange(experts, dtype=jnp.int32)
    member = jnp.any(ids_t[:, None, :] == names[None, :, None], axis=0)
    earlier = (jnp.arange(tok_rows)[:, None] < jnp.arange(tok_rows)[None, :]).astype(jnp.bfloat16)
    before = jnp.dot(member.astype(jnp.bfloat16), earlier, preferred_element_type=jnp.float32)
    slot = jnp.where(member, before.astype(jnp.int32), -1)

    wanted = jnp.arange(capacity, dtype=jnp.int32)
    logits = lax.dot_general(
        router_weight, tokens, (((0,), (1,)), ((), ())), preferred_element_type=jnp.float32
    )
    raised = jnp.where(member, jnp.exp(logits), 0.0)
    probs = raised / jnp.sum(raised, axis=0, keepdims=True)
    boxes = []
    for numbers in (wanted[:EARLY], wanted[EARLY:]):
        pick = (slot[:, None, :] == numbers[None, :, None]).reshape(-1, tok_rows)
        box = jnp.dot(pick.astype(jnp.bfloat16), tokens, preferred_element_type=jnp.float32)
        boxes.append(box.astype(jnp.bfloat16).reshape(experts, -1, model_width))
    first_box, last_box, probs, slot = lax.optimization_barrier((*boxes, probs, slot))

    early = exchange(first_box)
    early, last_box = lax.optimization_barrier((early, last_box))
    late = exchange(last_box)
    mats = (gate_weight[0], up_weight[0], down_weight[0])
    out = expert_apply(early, *mats, capacity, 0)
    out = expert_apply(late, *mats, capacity, EARLY // (capacity - EARLY), out)
    back = exchange(out)

    pick = slot[:, None, :] == wanted[None, :, None]
    table = table_of(back, cotangent, slot, probs)
    slot_grad = jnp.sum(jnp.where(pick, table[:, None, :], 0.0), axis=2)
    theirs = exchange(slot_grad[:, None, :])
    mixed = mixed_of(back, slot, probs)
    column = column_of(early, late, theirs.reshape(experts, capacity))
    column = column + lax.ppermute(column, "dp", [(0, 1), (1, 0)])
    columns = exchange(jnp.broadcast_to(column.astype(jnp.bfloat16), (experts,) + column.shape))
    columns = columns.reshape(experts, model_width)
    return (mixed, columns.astype(jnp.float32).T)


def solution(mesh):
    in_specs = (
        P(("dp", "expert", "replica"), None),
        P(("dp", "expert", "replica"), None),
        P(),
        P(("expert", "replica"), None, None),
        P(("expert", "replica"), None, None),
        P(("expert", "replica"), None, None),
        P(("dp", "expert", "replica"), None),
    )
    out_specs = (P(("dp", "expert", "replica"), None), P())
    return jax.shard_map(local, mesh=mesh, in_specs=in_specs, out_specs=out_specs, check_vma=False)
```

```python
import functools

import jax
import jax.numpy as jnp
from jax import lax
from jax.experimental import pallas as pl
from jax.experimental.pallas import tpu as pltpu
from jax.sharding import PartitionSpec as P

GROUP = ("expert", "replica")
EARLY = 16
STEP = 8
BLOCKS = 32
SPAN = 512
GROUPED = 32
PIECES = 16
SPANM = 2048


def exchange(rows):
    return lax.all_to_all(rows, GROUP, split_axis=0, concat_axis=0, tiled=True)


def expert_kernel(held, rows_ref, gate_hbm, up_hbm, down_hbm, *rest):
    out_refs = rest[held:-4]
    gate_mat, up_mat, down_mat, sems = rest[-4:]
    copies = [
        pltpu.make_async_copy(source, target, sems.at[n])
        for n, (source, target) in enumerate(
            ((gate_hbm, gate_mat), (up_hbm, up_mat), (down_hbm, down_mat))
        )
    ]
    first = pl.program_id(0) == 0

    @pl.when(first)
    def _():
        for copy in copies:
            copy.start()
        copies[0].wait()

    blocks, slots, width = rows_ref.shape
    flat = (blocks * slots, width)
    gate_act = jnp.dot(
        rows_ref[...].reshape(flat), gate_mat[...], preferred_element_type=jnp.float32
    )

    @pl.when(first)
    def _():
        copies[1].wait()

    up_act = jnp.dot(rows_ref[...].reshape(flat), up_mat[...], preferred_element_type=jnp.float32)
    hidden = (jax.nn.silu(gate_act) * up_act).astype(jnp.bfloat16)

    @pl.when(first)
    def _():
        copies[2].wait()

    for start in range(0, width, SPAN):
        part = jnp.dot(hidden, down_mat[:, start : start + SPAN], preferred_element_type=jnp.float32)
        part = part.reshape(blocks, slots, SPAN)
        for n, out_ref in enumerate(out_refs):
            out_ref[:, :, start : start + SPAN] = part[:, n * STEP : n * STEP + STEP].astype(jnp.bfloat16)


def expert_apply(rows, gate_mat, up_mat, down_mat, outs, into=None):
    sources, slots, width = rows.shape
    depth = gate_mat.shape[1]
    whole = pl.BlockSpec(memory_space=pl.ANY)
    held = [] if into is None else [into]
    return pl.pallas_call(
        functools.partial(expert_kernel, len(held)),
        out_shape=[jax.ShapeDtypeStruct((sources, n, width), jnp.bfloat16) for n, _ in outs],
        grid=(sources // BLOCKS,),
        in_specs=[pl.BlockSpec((BLOCKS, slots, width), lambda i: (i, 0, 0)), whole, whole, whole]
        + [whole] * len(held),
        out_specs=[
            pl.BlockSpec((BLOCKS, STEP, width), functools.partial(lambda place, i: (i, place, 0), place))
            for _, place in outs
        ],
        scratch_shapes=[
            pltpu.VMEM((width, depth), jnp.bfloat16),
            pltpu.VMEM((width, depth), jnp.bfloat16),
            pltpu.VMEM((depth, width), jnp.bfloat16),
            pltpu.SemaphoreType.DMA((3,)),
        ],
        input_output_aliases={4: 0} if held else {},
        compiler_params=pltpu.CompilerParams(vmem_limit_bytes=60 << 20),
        cost_estimate=pl.CostEstimate(
            flops=6 * sources * slots * width * depth,
            bytes_accessed=2 * (2 * sources * slots * width + 3 * width * depth),
            transcendentals=sources * slots * depth,
        ),
        name="experts",
    )(rows, gate_mat, up_mat, down_mat, *held)


def column_kernel(early_hbm, late_hbm, scale_ref, out_ref, early, late, total, sems):
    count = early.shape[0] // PIECES
    parts = ((early_hbm, early), (late_hbm, late))
    copies = []
    for n in range(PIECES):
        cut = pl.ds(n * count, count)
        copies.append(
            [
                pltpu.make_async_copy(source.at[cut], target.at[cut], sems.at[k, n])
                for k, (source, target) in enumerate(parts)
            ]
        )
    for pair in copies:
        for copy in pair:
            copy.start()
    first = early.shape[1]
    slots = first + late.shape[1]
    width = early.shape[2]
    for n, pair in enumerate(copies):
        scales = [
            jnp.broadcast_to(scale_ref[s][:, None], (slots, 128))
            for s in range(n * count, n * count + count)
        ]
        for copy in pair:
            copy.wait()
        for start in range(0, width, 128):
            lanes = slice(start, start + 128)
            part = []
            for s in range(count):
                row = n * count + s
                part.append(early[row, :, lanes].astype(jnp.float32) * scales[s][:first])
            while len(part) > 1:
                part = [a + b for a, b in zip(part[::2], part[1::2])]
            part = [part[0][k : k + 8] for k in range(0, first, 8)]
            for s in range(count):
                row = n * count + s
                part.append(late[row, :, lanes].astype(jnp.float32) * scales[s][first:])
            part = sum(part[1:], part[0])
            if n == 0:
                total[:, lanes] = part
            elif n < PIECES - 1:
                total[:, lanes] += part
            else:
                out_ref[start // 128 : start // 128 + 1, :] = jnp.sum(
                    total[:, lanes] + part, axis=0, keepdims=True
                )


def column_of(early, late, scales):
    width = early.shape[2]
    near = pl.BlockSpec(memory_space=pltpu.VMEM)
    whole = pl.BlockSpec(memory_space=pl.ANY)
    return pl.pallas_call(
        column_kernel,
        out_shape=jax.ShapeDtypeStruct((width // 128, 128), jnp.float32),
        in_specs=[whole, whole, near],
        out_specs=near,
        scratch_shapes=[
            pltpu.VMEM(early.shape, jnp.bfloat16),
            pltpu.VMEM(late.shape, jnp.bfloat16),
            pltpu.VMEM((late.shape[1], width), jnp.float32),
            pltpu.SemaphoreType.DMA((2, PIECES)),
        ],
        compiler_params=pltpu.CompilerParams(vmem_limit_bytes=60 << 20),
        name="column",
    )(early, late, scales)


def picked(slot, start, slots, values):
    blocks, rows = slot.shape
    wanted = start + lax.broadcasted_iota(jnp.int32, (blocks, slots, rows), 1)
    return jnp.where(slot[:, None, :] == wanted, values, 0.0)


def table_kernel(early_ref, late_ref, cotangent_ref, slot_ref, probs_ref, out_ref, dots):
    step = pl.program_id(0)
    rows = cotangent_ref.shape[0]
    slot = slot_ref[...]
    start = 0
    found = jnp.zeros(slot.shape, jnp.float32)
    for back_ref in (early_ref, late_ref):
        blocks, slots, width = back_ref.shape
        every = lax.dot_general(
            back_ref[...].reshape(blocks * slots, width),
            cotangent_ref[...],
            (((1,), (1,)), ((), ())),
            preferred_element_type=jnp.float32,
        ).reshape(blocks, slots, rows)
        found = found + jnp.sum(picked(slot, start, slots, every), axis=1)
        start += slots
    dots[pl.ds(pl.multiple_of(step * GROUPED, GROUPED), GROUPED), :] = found

    @pl.when(step == pl.num_programs(0) - 1)
    def _():
        probs = probs_ref[...]
        values = dots[...]
        out_ref[...] = probs * (values - jnp.sum(probs * values, axis=0, keepdims=True))


def table_of(early, late, cotangent, slot, probs):
    experts, rows = slot.shape
    width = cotangent.shape[1]
    return pl.pallas_call(
        table_kernel,
        out_shape=jax.ShapeDtypeStruct((experts, rows), jnp.float32),
        grid=(experts // GROUPED,),
        in_specs=[
            pl.BlockSpec((GROUPED, early.shape[1], width), lambda i: (i, 0, 0)),
            pl.BlockSpec((GROUPED, late.shape[1], width), lambda i: (i, 0, 0)),
            pl.BlockSpec((rows, width), lambda i: (0, 0)),
            pl.BlockSpec((GROUPED, rows), lambda i: (i, 0)),
            pl.BlockSpec((experts, rows), lambda i: (0, 0)),
        ],
        out_specs=pl.BlockSpec((experts, rows), lambda i: (0, 0)),
        scratch_shapes=[pltpu.VMEM((experts, rows), jnp.float32)],
        compiler_params=pltpu.CompilerParams(vmem_limit_bytes=60 << 20),
        name="table",
    )(early, late, cotangent, slot, probs)


def mixed_kernel(early_ref, late_ref, slot_ref, probs_ref, out_ref, early_share, late_share):
    rows = out_ref.shape[0]
    parts = ((early_ref, early_share), (late_ref, late_share))

    @pl.when(pl.program_id(0) == 0)
    def _():
        start = 0
        for back_ref, share in parts:
            blocks, slots, _ = back_ref.shape
            chosen = picked(slot_ref[...], start, slots, probs_ref[...][:, None, :])
            share[...] = chosen.reshape(blocks * slots, rows).T.astype(jnp.bfloat16)
            start += slots

    total = jnp.zeros(out_ref.shape, jnp.float32)
    for back_ref, share in parts:
        blocks, slots, width = back_ref.shape
        total = total + jnp.dot(
            share[...], back_ref[...].reshape(blocks * slots, width), preferred_element_type=jnp.float32
        )
    out_ref[...] = total.astype(jnp.bfloat16)


def mixed_of(early, late, slot, probs):
    experts, rows = slot.shape
    width = early.shape[2]
    tables = pl.BlockSpec((experts, rows), lambda i: (0, 0))
    return pl.pallas_call(
        mixed_kernel,
        out_shape=jax.ShapeDtypeStruct((rows, width), jnp.bfloat16),
        grid=(width // SPANM,),
        in_specs=[
            pl.BlockSpec((experts, early.shape[1], SPANM), lambda i: (0, 0, i)),
            pl.BlockSpec((experts, late.shape[1], SPANM), lambda i: (0, 0, i)),
            tables,
            tables,
        ],
        out_specs=pl.BlockSpec((rows, SPANM), lambda i: (0, i)),
        scratch_shapes=[
            pltpu.VMEM((rows, experts * early.shape[1]), jnp.bfloat16),
            pltpu.VMEM((rows, experts * late.shape[1]), jnp.bfloat16),
        ],
        compiler_params=pltpu.CompilerParams(vmem_limit_bytes=60 << 20),
        name="mixed",
    )(early, late, slot, probs)


def local(tokens, expert_ids, router_weight, gate_weight, up_weight, down_weight, cotangent):
    tok_rows, model_width = tokens.shape
    top_count = expert_ids.shape[1]
    experts = router_weight.shape[1]
    capacity = 3 * tok_rows * top_count // (2 * experts)
    ids_t = expert_ids.T
    names = jnp.arange(experts, dtype=jnp.int32)
    member = jnp.any(ids_t[:, None, :] == names[None, :, None], axis=0)
    earlier = (jnp.arange(tok_rows)[:, None] < jnp.arange(tok_rows)[None, :]).astype(jnp.bfloat16)
    before = jnp.dot(member.astype(jnp.bfloat16), earlier, preferred_element_type=jnp.float32)
    slot = jnp.where(member, before.astype(jnp.int32), -1)

    wanted = jnp.arange(capacity, dtype=jnp.int32)
    boxes = []
    for numbers in (wanted[:EARLY], wanted[EARLY:]):
        pick = (slot[:, None, :] == numbers[None, :, None]).reshape(-1, tok_rows)
        box = jnp.dot(pick.astype(jnp.bfloat16), tokens, preferred_element_type=jnp.float32)
        boxes.append(box.astype(jnp.bfloat16).reshape(experts, -1, model_width))
    first_box, last_box, slot = lax.optimization_barrier((*boxes, slot))

    early = exchange(first_box)
    early, last_box, member, router_weight = lax.optimization_barrier(
        (early, last_box, member, router_weight)
    )
    late = exchange(last_box)
    logits = lax.dot_general(
        router_weight, tokens, (((0,), (1,)), ((), ())), preferred_element_type=jnp.float32
    )
    raised = jnp.where(member, jnp.exp(logits), 0.0)
    probs = raised / jnp.sum(raised, axis=0, keepdims=True)
    mats = (gate_weight[0], up_weight[0], down_weight[0])
    out_early, out_late = expert_apply(early, *mats, ((STEP, 0), (capacity - STEP, 0)))
    late, out_early = lax.optimization_barrier((late, out_early))
    back_early = exchange(out_early)
    (out_late,) = expert_apply(late, *mats, ((capacity - STEP, 1),), out_late)
    back_early, out_late, probs = lax.optimization_barrier((back_early, out_late, probs))
    back_late = exchange(out_late)

    table = table_of(back_early, back_late, cotangent, slot, probs)
    pick = slot[:, None, :] == wanted[None, :, None]
    slot_grad = jnp.sum(jnp.where(pick, table[:, None, :], 0.0), axis=2)
    theirs = exchange(slot_grad[:, None, :])
    mixed = mixed_of(back_early, back_late, slot, probs)
    column = column_of(early, late, theirs.reshape(experts, capacity))
    column = column + lax.ppermute(column, "dp", [(0, 1), (1, 0)])
    columns = exchange(jnp.broadcast_to(column.astype(jnp.bfloat16), (experts,) + column.shape))
    columns = columns.reshape(experts, model_width)
    return (mixed, columns.astype(jnp.float32).T)


def solution(mesh):
    in_specs = (
        P(("dp", "expert", "replica"), None),
        P(("dp", "expert", "replica"), None),
        P(),
        P(("expert", "replica"), None, None),
        P(("expert", "replica"), None, None),
        P(("expert", "replica"), None, None),
        P(("dp", "expert", "replica"), None),
    )
    out_specs = (P(("dp", "expert", "replica"), None), P())
    return jax.shard_map(local, mesh=mesh, in_specs=in_specs, out_specs=out_specs, check_vma=False)
```

```python
import functools

import jax
import jax.numpy as jnp
from jax import lax
from jax.experimental import pallas as pl
from jax.experimental.pallas import tpu as pltpu
from jax.sharding import PartitionSpec as P

GROUP = ("expert", "replica")
EARLY = 16
STEP = 8
BLOCKS = 32
SPAN = 512
SPANT = 1024
PIECES = 16
SPANM = 2048


def exchange(rows):
    return lax.all_to_all(rows, GROUP, split_axis=0, concat_axis=0, tiled=True)


def expert_kernel(held, rows_ref, gate_hbm, up_hbm, down_hbm, *rest):
    out_refs = rest[held:-4]
    gate_mat, up_mat, down_mat, sems = rest[-4:]
    copies = [
        pltpu.make_async_copy(source, target, sems.at[n])
        for n, (source, target) in enumerate(
            ((gate_hbm, gate_mat), (up_hbm, up_mat), (down_hbm, down_mat))
        )
    ]
    first = pl.program_id(0) == 0

    @pl.when(first)
    def _():
        for copy in copies:
            copy.start()
        copies[0].wait()

    blocks, slots, width = rows_ref.shape
    flat = (blocks * slots, width)
    gate_act = jnp.dot(
        rows_ref[...].reshape(flat), gate_mat[...], preferred_element_type=jnp.float32
    )

    @pl.when(first)
    def _():
        copies[1].wait()

    up_act = jnp.dot(rows_ref[...].reshape(flat), up_mat[...], preferred_element_type=jnp.float32)
    hidden = (jax.nn.silu(gate_act) * up_act).astype(jnp.bfloat16)

    @pl.when(first)
    def _():
        copies[2].wait()

    for start in range(0, width, SPAN):
        part = jnp.dot(hidden, down_mat[:, start : start + SPAN], preferred_element_type=jnp.float32)
        part = part.reshape(blocks, slots, SPAN)
        for n, out_ref in enumerate(out_refs):
            out_ref[:, :, start : start + SPAN] = part[:, n * STEP : n * STEP + STEP].astype(jnp.bfloat16)


def expert_apply(rows, gate_mat, up_mat, down_mat, outs, into=None):
    sources, slots, width = rows.shape
    depth = gate_mat.shape[1]
    whole = pl.BlockSpec(memory_space=pl.ANY)
    held = [] if into is None else [into]
    return pl.pallas_call(
        functools.partial(expert_kernel, len(held)),
        out_shape=[jax.ShapeDtypeStruct((sources, n, width), jnp.bfloat16) for n, _ in outs],
        grid=(sources // BLOCKS,),
        in_specs=[pl.BlockSpec((BLOCKS, slots, width), lambda i: (i, 0, 0)), whole, whole, whole]
        + [whole] * len(held),
        out_specs=[
            pl.BlockSpec((BLOCKS, STEP, width), functools.partial(lambda place, i: (i, place, 0), place))
            for _, place in outs
        ],
        scratch_shapes=[
            pltpu.VMEM((width, depth), jnp.bfloat16),
            pltpu.VMEM((width, depth), jnp.bfloat16),
            pltpu.VMEM((depth, width), jnp.bfloat16),
            pltpu.SemaphoreType.DMA((3,)),
        ],
        input_output_aliases={4: 0} if held else {},
        compiler_params=pltpu.CompilerParams(vmem_limit_bytes=60 << 20),
        cost_estimate=pl.CostEstimate(
            flops=6 * sources * slots * width * depth,
            bytes_accessed=2 * (2 * sources * slots * width + 3 * width * depth),
            transcendentals=sources * slots * depth,
        ),
        name="experts",
    )(rows, gate_mat, up_mat, down_mat, *held)


def column_kernel(early_hbm, late_hbm, scale_ref, out_ref, early, late, total, sems):
    count = early.shape[0] // PIECES
    parts = ((early_hbm, early), (late_hbm, late))
    copies = []
    for n in range(PIECES):
        cut = pl.ds(n * count, count)
        copies.append(
            [
                pltpu.make_async_copy(source.at[cut], target.at[cut], sems.at[k, n])
                for k, (source, target) in enumerate(parts)
            ]
        )
    for pair in copies:
        for copy in pair:
            copy.start()
    first = early.shape[1]
    slots = first + late.shape[1]
    width = early.shape[2]
    for n, pair in enumerate(copies):
        scales = [
            jnp.broadcast_to(scale_ref[s][:, None], (slots, 128))
            for s in range(n * count, n * count + count)
        ]
        for copy in pair:
            copy.wait()
        for start in range(0, width, 128):
            lanes = slice(start, start + 128)
            part = []
            for s in range(count):
                row = n * count + s
                part.append(early[row, :, lanes].astype(jnp.float32) * scales[s][:first])
            while len(part) > 1:
                part = [a + b for a, b in zip(part[::2], part[1::2])]
            part = [part[0][k : k + 8] for k in range(0, first, 8)]
            for s in range(count):
                row = n * count + s
                part.append(late[row, :, lanes].astype(jnp.float32) * scales[s][first:])
            part = sum(part[1:], part[0])
            if n == 0:
                total[:, lanes] = part
            elif n < PIECES - 1:
                total[:, lanes] += part
            else:
                out_ref[start // 128 : start // 128 + 1, :] = jnp.sum(
                    total[:, lanes] + part, axis=0, keepdims=True
                )


def column_of(early, late, scales):
    width = early.shape[2]
    near = pl.BlockSpec(memory_space=pltpu.VMEM)
    whole = pl.BlockSpec(memory_space=pl.ANY)
    return pl.pallas_call(
        column_kernel,
        out_shape=jax.ShapeDtypeStruct((width // 128, 128), jnp.float32),
        in_specs=[whole, whole, near],
        out_specs=near,
        scratch_shapes=[
            pltpu.VMEM(early.shape, jnp.bfloat16),
            pltpu.VMEM(late.shape, jnp.bfloat16),
            pltpu.VMEM((late.shape[1], width), jnp.float32),
            pltpu.SemaphoreType.DMA((2, PIECES)),
        ],
        compiler_params=pltpu.CompilerParams(vmem_limit_bytes=60 << 20),
        name="column",
    )(early, late, scales)


def picked(slot, start, slots, values):
    blocks, rows = slot.shape
    wanted = start + lax.broadcasted_iota(jnp.int32, (blocks, slots, rows), 1)
    return jnp.where(slot[:, None, :] == wanted, values, 0.0)


def slot_grad_kernel(early_ref, late_ref, cotangent_ref, slot_ref, probs_ref, out_ref, early, late):
    step = pl.program_id(0)
    parts = ((early_ref, early), (late_ref, late))

    @pl.when(step == 0)
    def _():
        for _, total in parts:
            total[...] = jnp.zeros_like(total)

    for back_ref, total in parts:
        blocks, slots, width = back_ref.shape
        total[...] += lax.dot_general(
            back_ref[...].reshape(blocks * slots, width),
            cotangent_ref[...],
            (((1,), (1,)), ((), ())),
            preferred_element_type=jnp.float32,
        )

    @pl.when(step == pl.num_programs(0) - 1)
    def _():
        slot = slot_ref[...]
        probs = probs_ref[...]
        dots = jnp.zeros(slot.shape, jnp.float32)
        start = 0
        for back_ref, total in parts:
            blocks, slots, _ = back_ref.shape
            every = total[...].reshape(blocks, slots, slot.shape[1])
            dots = dots + jnp.sum(picked(slot, start, slots, every), axis=1)
            start += slots
        table = probs * (dots - jnp.sum(probs * dots, axis=0, keepdims=True))
        out_ref[...] = jnp.sum(picked(slot, 0, start, table[:, None, :]), axis=2)


def slot_grad_of(early, late, cotangent, slot, probs):
    experts, rows = slot.shape
    counts = (early.shape[1], late.shape[1])
    width = cotangent.shape[1]
    tables = pl.BlockSpec((experts, rows), lambda i: (0, 0))
    return pl.pallas_call(
        slot_grad_kernel,
        out_shape=jax.ShapeDtypeStruct((experts, sum(counts)), jnp.float32),
        grid=(width // SPANT,),
        in_specs=[pl.BlockSpec((experts, n, SPANT), lambda i: (0, 0, i)) for n in counts]
        + [pl.BlockSpec((rows, SPANT), lambda i: (0, i)), tables, tables],
        out_specs=pl.BlockSpec((experts, sum(counts)), lambda i: (0, 0)),
        scratch_shapes=[pltpu.VMEM((experts * n, rows), jnp.float32) for n in counts],
        compiler_params=pltpu.CompilerParams(vmem_limit_bytes=60 << 20),
        name="slot_grad",
    )(early, late, cotangent, slot, probs)


def mixed_kernel(early_ref, late_ref, slot_ref, probs_ref, out_ref, early_share, late_share):
    rows = out_ref.shape[0]
    parts = ((early_ref, early_share), (late_ref, late_share))

    @pl.when(pl.program_id(0) == 0)
    def _():
        start = 0
        for back_ref, share in parts:
            blocks, slots, _ = back_ref.shape
            chosen = picked(slot_ref[...], start, slots, probs_ref[...][:, None, :])
            share[...] = chosen.reshape(blocks * slots, rows).T.astype(jnp.bfloat16)
            start += slots

    total = jnp.zeros(out_ref.shape, jnp.float32)
    for back_ref, share in parts:
        blocks, slots, width = back_ref.shape
        total = total + jnp.dot(
            share[...], back_ref[...].reshape(blocks * slots, width), preferred_element_type=jnp.float32
        )
    out_ref[...] = total.astype(jnp.bfloat16)


def mixed_of(early, late, slot, probs):
    experts, rows = slot.shape
    width = early.shape[2]
    tables = pl.BlockSpec((experts, rows), lambda i: (0, 0))
    return pl.pallas_call(
        mixed_kernel,
        out_shape=jax.ShapeDtypeStruct((rows, width), jnp.bfloat16),
        grid=(width // SPANM,),
        in_specs=[
            pl.BlockSpec((experts, early.shape[1], SPANM), lambda i: (0, 0, i)),
            pl.BlockSpec((experts, late.shape[1], SPANM), lambda i: (0, 0, i)),
            tables,
            tables,
        ],
        out_specs=pl.BlockSpec((rows, SPANM), lambda i: (0, i)),
        scratch_shapes=[
            pltpu.VMEM((rows, experts * early.shape[1]), jnp.bfloat16),
            pltpu.VMEM((rows, experts * late.shape[1]), jnp.bfloat16),
        ],
        compiler_params=pltpu.CompilerParams(vmem_limit_bytes=60 << 20),
        name="mixed",
    )(early, late, slot, probs)


def local(tokens, expert_ids, router_weight, gate_weight, up_weight, down_weight, cotangent):
    tok_rows, model_width = tokens.shape
    top_count = expert_ids.shape[1]
    experts = router_weight.shape[1]
    capacity = 3 * tok_rows * top_count // (2 * experts)
    ids_t = expert_ids.T
    names = jnp.arange(experts, dtype=jnp.int32)
    member = jnp.any(ids_t[:, None, :] == names[None, :, None], axis=0)
    earlier = (jnp.arange(tok_rows)[:, None] < jnp.arange(tok_rows)[None, :]).astype(jnp.bfloat16)
    before = jnp.dot(member.astype(jnp.bfloat16), earlier, preferred_element_type=jnp.float32)
    slot = jnp.where(member, before.astype(jnp.int32), -1)

    wanted = jnp.arange(capacity, dtype=jnp.int32)
    boxes = []
    for numbers in (wanted[:EARLY], wanted[EARLY:]):
        pick = (slot[:, None, :] == numbers[None, :, None]).reshape(-1, tok_rows)
        box = jnp.dot(pick.astype(jnp.bfloat16), tokens, preferred_element_type=jnp.float32)
        boxes.append(box.astype(jnp.bfloat16).reshape(experts, -1, model_width))
    first_box, last_box, slot = lax.optimization_barrier((*boxes, slot))

    early = exchange(first_box)
    early, last_box, member, router_weight = lax.optimization_barrier(
        (early, last_box, member, router_weight)
    )
    late = exchange(last_box)
    logits = lax.dot_general(
        router_weight, tokens, (((0,), (1,)), ((), ())), preferred_element_type=jnp.float32
    )
    raised = jnp.where(member, jnp.exp(logits), 0.0)
    probs = raised / jnp.sum(raised, axis=0, keepdims=True)
    mats = (gate_weight[0], up_weight[0], down_weight[0])
    out_early, out_late = expert_apply(early, *mats, ((STEP, 0), (capacity - STEP, 0)))
    late, out_early = lax.optimization_barrier((late, out_early))
    back_early = exchange(out_early)
    (out_late,) = expert_apply(late, *mats, ((capacity - STEP, 1),), out_late)
    back_early, out_late, probs = lax.optimization_barrier((back_early, out_late, probs))
    back_late = exchange(out_late)

    slot_grad = slot_grad_of(back_early, back_late, cotangent, slot, probs)
    theirs = exchange(slot_grad[:, None, :])
    mixed = mixed_of(back_early, back_late, slot, probs)
    column = column_of(early, late, theirs.reshape(experts, capacity))
    column = column + lax.ppermute(column, "dp", [(0, 1), (1, 0)])
    columns = exchange(jnp.broadcast_to(column.astype(jnp.bfloat16), (experts,) + column.shape))
    columns = columns.reshape(experts, model_width)
    return (mixed, columns.astype(jnp.float32).T)


def solution(mesh):
    in_specs = (
        P(("dp", "expert", "replica"), None),
        P(("dp", "expert", "replica"), None),
        P(),
        P(("expert", "replica"), None, None),
        P(("expert", "replica"), None, None),
        P(("expert", "replica"), None, None),
        P(("dp", "expert", "replica"), None),
    )
    out_specs = (P(("dp", "expert", "replica"), None), P())
    return jax.shard_map(local, mesh=mesh, in_specs=in_specs, out_specs=out_specs, check_vma=False)
```
